32 devices in a mesh: kpt: 2 (over y), pert: 4 (over z), pw: 4 (over x, core).
Axes of the slice: x: 2, y: 2, z: 4, core: 2. Of those that a mesh axis runs over, the one named last changes fastest.
Arguments:
- occupied: bfloat16 [3072, 8192], P(('kpt', 'pert'), 'pw'), parts along dimension 0, may hold values from -0.0625 to 0.0625
- response: bfloat16 [8, 128, 8192], P(('kpt', 'pert'), None, 'pw'), parts along dimension 0, may hold values from -6 to 6
Outputs:
- correlation: float32 [8, 128, 1536], P(('kpt', 'pert')), parts along dimension 0
- projected: float32 [8, 128, 8192], P(('kpt', 'pert'), None, 'pw'), parts along dimension 0
The draws below stay inside these ranges and needn't reach their ends.
There are 2 independent parts, one for each index of `kpt`. The reference program is written for one: setup_inputs(seed, part) draws one part's arguments, and reference() takes and returns one part's arrays. A program takes and returns all parts, laid end to end along the dimension named above; each array names one. Nothing has to cross between parts.
All inputs are finite; a program needn't handle non-finite values.
Results may differ from the reference program's by a relative error of at most 0.00096.
Values may be sent and summed in bfloat16 or wider, within the bound.
No kernel may reach another device: no remote copies, remote signals or barrier semaphores. Data moves between devices by JAX's collectives and lax.ppermute only.
A program may use at most 64 MiB of HBM per device.

```python
import jax
import jax.numpy as jnp
from jax import lax

NB = 1536
RB = 128
NPW = 8192
NPERT = 4


def steps_of(own_key, shape, split, low, largest):
    def one(axis_at, shards_of):
        steps = jax.random.uniform(jax.random.fold_in(jax.random.fold_in(own_key, 6), axis_at), (shards_of,), jnp.float32, low / len(split), largest / len(split))
        return jnp.repeat(jnp.exp(steps), shape[axis_at] // shards_of).reshape((-1,) + (1,) * (len(shape) - axis_at - 1))

    gain = one(*split[0])
    for cut in split[1:]:
        gain = gain * one(*cut)
    return gain


def centred(stream_key, extent, spread, bound, pieces=(), dtype=jnp.bfloat16):
    drawn = spread * jax.random.normal(stream_key, extent, jnp.float32)
    if pieces:
        drawn = drawn * steps_of(stream_key, extent, pieces, -0.22, 0.18)
    return jnp.clip(drawn, -bound, bound).astype(dtype)


def setup_inputs(seed: int = 0, part: int = 0) -> dict:
    seeds = jax.random.split(jax.random.key(seed), 3)
    own_keys = jax.random.split(jax.random.fold_in(seeds[2], part), 3)
    occupied = centred(own_keys[0], (NB, NPW), NPW ** -0.5, 0.0625, ((0, 4), (1, 4)))
    response = centred(own_keys[1], (NPERT, RB, NPW), 1.0, 6.0, ((0, 4), (2, 4)))
    return {"occupied": occupied, "response": response}


def reference(occupied, response):
    def one_perturbation(resp):
        correlation = lax.dot_general(resp, occupied, (((1,), (1,)), ((), ())), preferred_element_type=jnp.float32)
        weights = correlation.astype(jnp.bfloat16)
        correction = jnp.dot(weights, occupied, preferred_element_type=jnp.float32)
        return correlation, resp.astype(jnp.float32) - correction

    correlation, projected = lax.map(one_perturbation, response)
    return correlation, projected
```

```python
import jax
import jax.numpy as jnp
from jax import lax
from jax.sharding import PartitionSpec as P


def shifted(block, axis, distance):
    size = lax.axis_size(axis)
    return lax.ppermute(block, axis, [(i, (i + distance) % size) for i in range(size)])


def partner(block, axis, mask):
    size = lax.axis_size(axis)
    return lax.ppermute(block, axis, [(i, i ^ mask) for i in range(size)])


def masks_of(size):
    return [1 << k for k in range(size.bit_length() - 1)]


def total(block, axis):
    size = lax.axis_size(axis)
    if size & (size - 1):
        return lax.psum(block, axis)
    for mask in masks_of(size):
        block = block + partner(block, axis, mask)
    return block


def local(occupied, response):
    rows = response.reshape(-1, response.shape[-1])
    height = rows.shape[0]
    bands = occupied.shape[0]
    ring = lax.axis_size("pert")
    slabs = lax.axis_size("pw")
    here = lax.axis_index("pert")
    slab = lax.axis_index("pw")

    def correlate(block):
        part = lax.dot_general(
            block, occupied, (((1,), (1,)), ((), ())), preferred_element_type=jnp.float32
        )
        largest = jnp.max(jnp.abs(block)).astype(jnp.float32)
        both = jnp.concatenate([part, jnp.full((8, bands), largest)], axis=0)
        both = total(both, "pw")
        return both[:height], both[height, 0]

    def correct(correlation):
        return jnp.dot(
            correlation.astype(jnp.bfloat16), occupied, preferred_element_type=jnp.float32
        )

    plane_waves = slabs * rows.shape[1]
    bound = bands * ring * plane_waves / 256.0 / 32768.0

    def factor(size):
        return jnp.where(size > 0, size, 1.0) * bound

    blocks = [rows]
    for _ in range(ring - 1):
        blocks.append(shifted(blocks[-1], "pert", 1))
    found = [correlate(block) for block in blocks]

    piece = height // slabs
    quarter = [lax.dynamic_slice_in_dim(c, slab * piece, piece, 0) for c, _ in found]
    gathered = jnp.zeros((piece, ring * bands), jnp.float32)
    for step in range(ring):
        got = quarter[step] if step == 0 else shifted(quarter[step], "pert", -step)
        gathered = lax.dynamic_update_slice(
            gathered, got, (jnp.zeros((), jnp.int32), (here + step) % ring * bands)
        )
    correlation = jnp.zeros((height, ring * bands), jnp.float32)
    correlation = lax.dynamic_update_slice_in_dim(correlation, gathered, slab * piece, 0)
    correlation = total(correlation, "pw") if slabs & (slabs - 1) else spread(gathered, slab, slabs)

    running = None
    for step in range(1, ring):
        c, size = found[step]
        added = correct(c) / factor(size)
        if running is not None:
            added = added + running.astype(jnp.float32)
        running = shifted(added.astype(jnp.float16), "pert", 1)
    correction = correct(found[0][0])
    if running is not None:
        correction = correction + running.astype(jnp.float32) * factor(found[0][1])
    projected = rows.astype(jnp.float32) - correction
    return (
        correlation.reshape(response.shape[0], response.shape[1], ring * bands),
        projected.reshape(response.shape),
    )


def spread(block, slab, slabs):
    for mask in masks_of(slabs):
        other = partner(block, "pw", mask)
        low = (slab & mask) == 0
        block = jnp.concatenate(
            [jnp.where(low, block, other), jnp.where(low, other, block)], axis=0
        )
    return block


def solution(mesh):
    in_specs = (P(("kpt", "pert"), "pw"), P(("kpt", "pert"), None, "pw"))
    out_specs = (P(("kpt", "pert"), None, None), P(("kpt", "pert"), None, "pw"))
    return jax.shard_map(local, mesh=mesh, in_specs=in_specs, out_specs=out_specs, check_vma=False)
```
